32 devices in a mesh: tp: 2 (over x), ad: 16 (over z, y, core).
Axes of the slice: x: 2, y: 2, z: 4, core: 2. Of those that a mesh axis runs over, the one named last changes fastest.
Arguments:
- tokens: bfloat16 [16384, 8192], P('ad', 'tp'), may hold values from -6 to 6
- value_weight: bfloat16 [8192, 1024], P(('tp', 'ad')), may hold values from -0.0625 to 0.0625
- adapter_down: bfloat16 [32, 8192, 128], P('ad', 'tp'), may hold values from -0.0625 to 0.0625
- adapter_up_panels: bfloat16 [32, 128, 1024], P('ad', None, 'tp'), may hold values from -0.5 to 0.5
- req_start: int32 [16], replicated, may hold values from 0 to 16128, as said below
- req_adapter: int32 [16], replicated, may hold values from 0 to 31
- adapter_home: int32 [32], replicated, may hold values from 0 to 31, each once
Outputs:
- adapted: bfloat16 [16384, 1024], P('ad', 'tp')
The draws below stay inside these ranges and needn't reach their ends.
Inputs may be any that keep to these rules, and one draw needn't show every extreme that they name: `req_start`: entries rise strictly, the first is 0 and each is a multiple of 256; the tokens of one index of ad meet at most 4 requests, and those of the first index meet exactly 4. Each storage row once; adapter a is stored on index adapter_home[a] // 2 of ad.
All inputs are finite; a program needn't handle non-finite values.
Results may differ from the reference program's by a relative error of at most 0.0085.
Values may be sent and summed in bfloat16 or wider, within the bound.
No kernel may reach another device: no remote copies, remote signals or barrier semaphores. Data moves between devices by JAX's collectives and lax.ppermute only.
A program may use at most 64 MiB of HBM per device.

```python
import math
import jax
import jax.numpy as jnp
import numpy as np
from jax import lax

D = 8192
KV = 1024
R = 128
TOK_DEV = 1024
FMAX = 4
REQS = 16
ADAPTERS = 32
TOKENS = 16384


def draw_req_start(key, part):
    block_rows = TOK_DEV // FMAX
    block_count = TOKENS // block_rows
    shuffled = jax.random.permutation(key, block_count - FMAX - 1) + FMAX
    picked = jnp.sort(shuffled[:REQS - FMAX - 1])
    starts = jnp.concatenate([jnp.arange(FMAX, dtype=jnp.int32), picked.astype(jnp.int32), jnp.full((1,), block_count - 1, jnp.int32)])
    return (starts * block_rows).astype(jnp.int32)


def plant(array, stream_key, low, high):
    longest = array.shape.index(max(array.shape))
    spots = []
    for shift in (0, 1):
        where = [jax.random.randint(jax.random.fold_in(stream_key, axis), (), 0, length) for axis, length in enumerate(array.shape)]
        where[longest] = (where[longest] + shift) % array.shape[longest]
        spots.append(tuple(where))
    return array.at[spots[0]].set(low).at[spots[1]].set(high)


def shard_levels(key, dims, cuts, low, top_value):
    gain, own = 1.0, jax.random.fold_in(key, 6)
    for axis_at, shards_of in cuts:
        steps = jnp.exp(jax.random.uniform(jax.random.fold_in(own, axis_at), (shards_of,), jnp.float32, low / len(cuts), top_value / len(cuts)))
        gain = gain * jnp.repeat(steps, dims[axis_at] // shards_of).reshape([-1 if axis == axis_at else 1 for axis in range(len(dims))])
    return gain


def rank_table(count, lean):
    loads = [(1 << 20) // math.isqrt(grade ** lean) + 1 for grade in range(1, count + 1)]
    scale = 1 + sum(loads) // (1 << 30)
    return np.cumsum(np.array([max(1, weight // scale) for weight in loads]))


def ranked_ids(stream_key, shape, count, skew):
    grid = rank_table(count, skew)
    pick = jax.random.randint(jax.random.fold_in(stream_key, 1), shape, 0, int(grid[count - 1]))
    rank = jnp.searchsorted(jnp.asarray(grid, jnp.int32), pick, side="right")
    return jax.random.permutation(jax.random.fold_in(stream_key, 2), count)[rank].astype(jnp.int32)


def scatter_about(own_key, dims, scale, reach, shards=(), kind=jnp.bfloat16):
    result = jax.random.normal(own_key, dims, jnp.float32) * scale
    if len(shards) > 0:
        result = shard_levels(own_key, dims, shards, -0.22, 0.18) * result
    return jnp.clip(result, min=-reach, max=reach).astype(kind)


def setup_inputs(seed: int = 0) -> dict:
    streams_of = jax.random.split(jax.random.key(seed), 8)
    tokens = scatter_about(streams_of[0], (TOKENS, D), 1.0, 6.0, ((0, 16), (1, 2)))
    value_weight = scatter_about(streams_of[1], (D, KV), D ** -0.5, 0.0625, ((0, 32),))
    adapter_down = scatter_about(streams_of[2], (ADAPTERS, D, R), D ** -0.5, 0.0625, ((0, 16), (1, 2)))
    adapter_up_panels = scatter_about(streams_of[3], (ADAPTERS, R, KV), R ** -0.5, 0.5, ((0, 16), (2, 2)))
    req_start = draw_req_start(jax.random.fold_in(streams_of[7], 71), 0)
    req_adapter = plant(ranked_ids(streams_of[5], (REQS,), ADAPTERS, 2), jax.random.fold_in(streams_of[5], 3), 0, ADAPTERS - 1).astype(jnp.int32)
    adapter_home = jax.random.permutation(streams_of[6], ADAPTERS).astype(jnp.int32)
    return {"tokens": tokens, "value_weight": value_weight, "adapter_down": adapter_down, "adapter_up_panels": adapter_up_panels, "req_start": req_start, "req_adapter": req_adapter, "adapter_home": adapter_home}


adapter_scale = 2.0


def reference(tokens, value_weight, adapter_down, adapter_up_panels, req_start, req_adapter, adapter_home):
    block_rows = TOK_DEV // FMAX
    blocks = TOKENS // block_rows
    first_rows = jnp.arange(blocks, dtype=jnp.int32) * block_rows
    request = jnp.sum((req_start[None, :] <= first_rows[:, None]).astype(jnp.int32), axis=1) - 1
    adapter = req_adapter[request.astype(jnp.int32)]
    stored = adapter_home[adapter.astype(jnp.int32)].astype(jnp.int32)
    tok_blocks = tokens.reshape(blocks, block_rows, D)

    def one_block(block_args):
        row_block, storage_row_index = block_args
        base_value_output = jnp.dot(row_block, value_weight, preferred_element_type=jnp.float32)
        down_panel = adapter_down[storage_row_index]
        adapter_rank_rows = jnp.dot(row_block, down_panel, preferred_element_type=jnp.float32).astype(jnp.bfloat16)
        adapter_value_delta = jnp.dot(adapter_rank_rows, adapter_up_panels[storage_row_index], preferred_element_type=jnp.float32)
        return (base_value_output + adapter_scale * adapter_value_delta).astype(jnp.bfloat16)

    adapted = lax.map(one_block, (tok_blocks, stored))
    return adapted.reshape(TOKENS, KV)
```

```python
import functools

import jax
import jax.numpy as jnp
from jax import lax
from jax.experimental import pallas as pl
from jax.experimental.pallas import tpu as pltpu
from jax.sharding import Mesh
from jax.sharding import PartitionSpec as P

FMAX = 4
LANES = 128

adapter_scale = 2.0
BF = jnp.bfloat16
F32 = jnp.float32


def swap(array, axis):
    return lax.ppermute(array, axis, [(0, 1), (1, 0)])


def rotate(array, axis, shift):
    count = lax.axis_size(axis)
    return lax.ppermute(array, axis, [(i, (i + shift) % count) for i in range(count)])


def base_kernel(zn, order, tok, *refs):
    pieces, out, acc = refs[:4], refs[4], refs[5]
    step = pl.program_id(0)

    @pl.when(step == 0)
    def _():
        acc[...] = jnp.zeros_like(acc)

    for g in range(4):

        @pl.when(step // zn == g)
        def _(g=g):
            acc[...] += jnp.dot(tok[...], pieces[g][0], preferred_element_type=F32)

    @pl.when(step == 4 * zn - 1)
    def _():
        out[...] = acc[...].astype(out.dtype)


def base_product(tokens, pieces, order, dtype):
    rows, width = tokens.shape
    zn, depth, cols = pieces[0].shape
    if depth % LANES:
        whole = jnp.stack(pieces)
        inverse = jnp.sum(jnp.where(order[None, :] == jnp.arange(4)[:, None], jnp.arange(4)[None, :], 0), axis=1)
        whole = jnp.take(whole, inverse, axis=0)
        whole = whole.transpose(1, 0, 2, 3).reshape(width, cols)
        return jnp.dot(tokens, whole, preferred_element_type=F32).astype(dtype)
    return pl.pallas_call(
        functools.partial(base_kernel, zn),
        out_shape=jax.ShapeDtypeStruct((rows, cols), dtype),
        grid_spec=pltpu.PrefetchScalarGridSpec(
            num_scalar_prefetch=1,
            grid=(4 * zn,),
            in_specs=[pl.BlockSpec((rows, depth), lambda i, o: (0, (i % zn) * 4 + o[i // zn]))]
            + [
                pl.BlockSpec((1, depth, cols), lambda i, o, g=g: (jnp.clip(i - g * zn, 0, zn - 1), 0, 0))
                for g in range(4)
            ],
            out_specs=pl.BlockSpec((rows, cols), lambda i, o: (0, 0)),
            scratch_shapes=[pltpu.VMEM((rows, cols), F32)],
        ),
        cost_estimate=pl.CostEstimate(
            flops=2 * rows * width * cols,
            bytes_accessed=2 * (rows * width + width * cols + rows * cols),
            transcendentals=0,
        ),
    )(order, tokens, *pieces)


def rank_kernel(quarter, order, slot, tok, *refs):
    panels, out = refs[:4], refs[4]
    total = None
    for g in range(4):
        first = pl.multiple_of(order[g] * quarter, LANES)
        part = jnp.dot(tok[:, pl.ds(first, quarter)], panels[g][0], preferred_element_type=F32)
        total = part if total is None else total + part
    out[...] = total


def rank_product(tokens, panels, order, slot, quarter, block_rows):
    rows, width = tokens.shape
    lanes = panels[0].shape[2]
    return pl.pallas_call(
        functools.partial(rank_kernel, quarter),
        out_shape=jax.ShapeDtypeStruct((rows, lanes), F32),
        grid_spec=pltpu.PrefetchScalarGridSpec(
            num_scalar_prefetch=2,
            grid=(rows // block_rows,),
            in_specs=[pl.BlockSpec((block_rows, width), lambda b, o, s: (b, 0))]
            + [pl.BlockSpec((1, quarter, lanes), lambda b, o, s: (s[b], 0, 0))] * 4,
            out_specs=pl.BlockSpec((block_rows, lanes), lambda b, o, s: (b, 0)),
        ),
        cost_estimate=pl.CostEstimate(
            flops=2 * rows * width * lanes, bytes_accessed=2 * rows * width + 4 * rows * lanes, transcendentals=0
        ),
    )(order, slot, tokens, *panels)


def final_kernel(others, up_rank, order, slot, rank, base, *refs):
    rank_got, base_got = refs[:others], refs[others : 2 * others]
    panels, out, up = refs[2 * others : 2 * others + 4], refs[2 * others + 4], refs[2 * others + 5]
    full = rank[...]
    value = base[...]
    for j in range(others):
        full += rank_got[j][...].astype(F32)
        value += base_got[j][...].astype(F32)
    for g in range(4):
        first = pl.multiple_of(order[g] * up_rank, up_rank)
        for c in range(out.shape[1] // LANES):
            up[pl.ds(first, up_rank), c * LANES : (c + 1) * LANES] = panels[g][0, c * up_rank : (c + 1) * up_rank, :]
    delta = jnp.dot(full.astype(BF), up[...], preferred_element_type=F32)
    out[...] = (value + adapter_scale * delta).astype(out.dtype)


def final_sum(rank, rank_got, base, base_got, panels, order, slot, quarter, block_rows):
    rows, cols = base.shape
    rank_width = rank.shape[1]
    up_rank = rank_width // 4
    up_rows = panels[0].shape[1] - quarter
    others = len(rank_got)
    return pl.pallas_call(
        functools.partial(final_kernel, others, up_rank),
        out_shape=jax.ShapeDtypeStruct((rows, cols), BF),
        grid_spec=pltpu.PrefetchScalarGridSpec(
            num_scalar_prefetch=2,
            grid=(rows // block_rows,),
            in_specs=[pl.BlockSpec((block_rows, rank_width), lambda b, o, s: (b, 0))]
            + [pl.BlockSpec((block_rows, cols), lambda b, o, s: (b, 0))]
            + [pl.BlockSpec((block_rows, rank_width), lambda b, o, s: (b, 0))] * others
            + [pl.BlockSpec((block_rows, cols), lambda b, o, s: (b, 0))] * others
            + [pl.BlockSpec((1, up_rows, LANES), lambda b, o, s: (s[b], quarter // up_rows, 0))] * 4,
            out_specs=pl.BlockSpec((block_rows, cols), lambda b, o, s: (b, 0)),
            scratch_shapes=[pltpu.VMEM((rank_width, cols), BF)],
        ),
        cost_estimate=pl.CostEstimate(
            flops=2 * rows * rank_width * cols, bytes_accessed=8 * rows * cols, transcendentals=0
        ),
    )(order, slot, rank, base, *rank_got, *base_got, *panels)


def gather_columns(weight, zn):
    copies = jnp.broadcast_to(weight[None], (zn, *weight.shape))
    along_z = lax.all_to_all(copies, "z", split_axis=0, concat_axis=0, tiled=True)
    along_y = swap(along_z, "y")
    return [along_z, along_y, swap(along_z, "c"), swap(along_y, "c")]


def body(tokens, value_weight, adapter_down, adapter_up, req_start, req_adapter, adapter_home):
    rows, width = tokens.shape
    tp = lax.axis_size("tp")
    zn = lax.axis_size("z")
    owned, _, rank_width = adapter_down.shape
    cols = adapter_up.shape[2]
    block_rows = rows // FMAX
    quarter = width // 4
    zi, yi, ci, ti = (lax.axis_index(a) for a in ("z", "y", "c", "tp"))
    here = 4 * owned
    total = zn * here

    i32 = jnp.int32
    block_first = jnp.arange(zn * 4 * FMAX, dtype=i32) * block_rows
    request = jnp.sum((req_start[None, :] <= block_first[:, None]).astype(i32), axis=1) - 1
    req_ids = jnp.arange(req_start.shape[0], dtype=i32)
    adapter = jnp.sum(jnp.where(request[:, None] == req_ids[None, :], req_adapter[None, :], 0), axis=1)
    ids = jnp.arange(total, dtype=i32)
    stored = jnp.sum(jnp.where(adapter[:, None] == ids[None, :], adapter_home[None, :], 0), axis=1)
    uses = (stored[:, None] == ids[None, :]).astype(i32)
    chip_uses = jnp.max(uses.reshape(zn * 2, 2 * FMAX, total), axis=1)
    z_uses = jnp.max(chip_uses.reshape(zn, 2, total), axis=1)
    pair_uses = z_uses.reshape(zn, zn, here)
    most_pair = jnp.max(jnp.sum(pair_uses, axis=2))
    most_chip = jnp.max(jnp.sum(chip_uses, axis=1))

    order_y = jnp.stack([yi, 1 - yi, yi, 1 - yi])
    order_c = jnp.stack([ci, ci, 1 - ci, 1 - ci])
    order = (order_y * 2 + order_c).astype(i32)

    down = adapter_down.reshape(owned, 4, quarter, rank_width)
    up = adapter_up.reshape(owned, 4, rank_width // 4, cols // LANES, LANES).transpose(0, 1, 3, 2, 4)
    up = up.reshape(owned, 4, -1, LANES)
    slab = jnp.concatenate([down, up], axis=2).transpose(1, 0, 2, 3)
    slab = lax.all_to_all(slab, ("y", "c"), split_axis=0, concat_axis=0, tiled=True)
    slab = slab.reshape(here, *slab.shape[2:])

    def run(limit_pair, limit_chip, slab, tokens, value_weight, chip_uses, pair_uses, uses):
        before = (jnp.arange(here)[:, None] > jnp.arange(here)[None, :]).astype(i32)
        place = jnp.sum(pair_uses[:, :, None, :] * before[None, None], axis=3)
        mine = (jnp.arange(zn) == zi).astype(i32)
        sent_uses = jnp.sum(pair_uses * mine[None, :, None], axis=1)
        sent_place = jnp.sum(place * mine[None, :, None], axis=1)
        hit = (sent_place[:, None, :] == jnp.arange(limit_pair)[None, :, None]) * sent_uses[:, None, :]
        send = jnp.sum(hit * jnp.arange(here)[None, None, :], axis=2)
        got_place = jnp.sum(place * mine[:, None, None], axis=0).reshape(total)
        got_at = (ids // here) * limit_pair + got_place
        earlier = (ids[:, None] > ids[None, :]).astype(i32)
        chip = zi * 2 + jnp.stack([yi, 1 - yi])
        both = jnp.sum(chip_uses[None] * (jnp.arange(zn * 2)[None, :] == chip[:, None])[:, :, None], axis=1)
        both_place = jnp.sum(both[:, None, :] * earlier[None], axis=2)
        hit = (both_place[:, None, :] == jnp.arange(limit_chip)[None, :, None]) * both[:, None, :]
        pick = jnp.sum(hit * got_at[None, None, :], axis=2)
        my_blocks = (zi * 4 + yi * 2 + ci) * FMAX + jnp.arange(FMAX)
        my_uses = jnp.sum(uses[None] * (jnp.arange(uses.shape[0])[None, :] == my_blocks[:, None])[:, :, None], axis=1)
        slot = jnp.sum(my_uses * both_place[0][None, :], axis=1).astype(i32)

        sent = []
        pieces = [
            gather_columns(
                lax.dynamic_slice_in_dim(value_weight, lax.rem(ti + shift, tp) * cols, cols, 1), zn
            )
            for shift in range(1, tp)
        ]
        own_pieces = gather_columns(lax.dynamic_slice_in_dim(value_weight, ti * cols, cols, 1), zn)

        out = jnp.take(slab, send.reshape(-1), axis=0).reshape(zn, limit_pair, *slab.shape[1:])
        got = lax.all_to_all(out, "z", split_axis=0, concat_axis=0, tiled=True)
        got = got.reshape(zn * limit_pair, *slab.shape[1:])
        own_part = jnp.take(got, pick[0], axis=0)
        y_part = swap(jnp.take(got, pick[1], axis=0), "y")
        panels = [own_part, y_part, swap(own_part, "c"), swap(y_part, "c")]

        for shift in range(1, tp):
            part = base_product(tokens, pieces[shift - 1], order, BF)
            sent.append(rotate(part, "tp", shift))
        base = base_product(tokens, own_pieces, order, F32)
        rank = rank_product(tokens, panels, order, slot, quarter, block_rows)
        rank_sent = [rotate(rank.astype(BF), "tp", shift) for shift in range(1, tp)]
        return final_sum(rank, rank_sent, base, sent, panels, order, slot, quarter, block_rows)

    tiers = [(2, 5), (3, 5), (4, 6), (here, 2 * FMAX)]
    fits = [(most_pair <= n) & (most_chip <= c) for n, c in tiers[:-1]]
    tier = jnp.int32(len(tiers) - 1)
    for level in reversed(range(len(fits))):
        tier = jnp.where(fits[level], level, tier)
    return lax.switch(
        tier,
        [functools.partial(run, n, c) for n, c in tiers],
        slab, tokens, value_weight, chip_uses, pair_uses, uses,
    )


def solution(mesh):
    tp, ad = mesh.shape["tp"], mesh.shape["ad"]
    fine = Mesh(mesh.devices.reshape(tp, ad // 4, 2, 2), ("tp", "z", "y", "c"))
    at = ("z", "y", "c")
    return jax.shard_map(
        body,
        mesh=fine,
        in_specs=(
            P(at, "tp"),
            P(("tp",) + at, None),
            P(at, "tp", None),
            P(at, None, "tp"),
            P(),
            P(),
            P(),
        ),
        out_specs=P(at, "tp"),
        check_vma=False,
    )
```

```python
import functools

import jax
import jax.numpy as jnp
from jax import lax
from jax.experimental import pallas as pl
from jax.experimental.pallas import tpu as pltpu
from jax.sharding import Mesh
from jax.sharding import PartitionSpec as P

FMAX = 4
LANES = 128
UNROLLED = (4, 5, 6)

adapter_scale = 2.0
BF = jnp.bfloat16
F32 = jnp.float32
I32 = jnp.int32


def swap(array, axis):
    return lax.ppermute(array, axis, [(0, 1), (1, 0)])


def rotate(array, axis, shift):
    count = lax.axis_size(axis)
    return lax.ppermute(array, axis, [(i, (i + shift) % count) for i in range(count)])


def step_z(array, direction):
    count = lax.axis_size("z")
    pairs = [(i, i + 1) for i in range(count - 1)]
    return lax.ppermute(array, "z", pairs if direction == 0 else [(b, a) for a, b in pairs])


class Plan:
    def __init__(self, zn, owned, requests, block_rows):
        self.zn, self.owned, self.requests, self.block_rows = zn, owned, requests, block_rows
        self.chip_owned = 2 * owned
        self.adapters = zn * 2 * self.chip_owned
        self.blocks = zn * 4 * FMAX
        self.steps = min(requests, self.adapters) + zn + 2 * FMAX + 4
        self.trash = self.chip_owned + min(requests, self.adapters)
        self.slots = self.trash + 1
        self.own_at = 6 * self.steps
        self.partner_at = self.own_at + FMAX
        self.rounds_at = self.partner_at + FMAX
        self.size = self.rounds_at + 1


def table_kernel(plan, start, adapter, home, me, out, stored, need, low, high, rank, sched, cnt):
    zn, steps, per_chip = plan.zn, plan.steps, plan.chip_owned
    total, requests = plan.adapters, plan.requests
    zi, yi, ci = me[0], me[1], me[2]

    def each(count, body):
        lax.fori_loop(0, count, lambda i, c: (body(i), c)[1], 0)

    def clear(s):
        low[s] = zn
        high[s] = -1

    each(total, clear)
    each(2 * zn * total, lambda i: need.__setitem__(i, 0))
    each(6 * zn * steps, lambda i: sched.__setitem__(i, -1))

    def block(b, r):
        following = jnp.minimum(r + 1, requests - 1)
        r = jnp.where((r + 1 < requests) & (start[following] <= b * plan.block_rows), r + 1, r)
        s = home[adapter[r]]
        stored[b] = s
        z = b // (4 * FMAX)
        low[s] = jnp.minimum(low[s], z)
        high[s] = jnp.maximum(high[s], z)
        need[(b // (2 * FMAX)) * total + s] = 1
        return r

    lax.fori_loop(0, plan.blocks, block, 0)

    def number(s, count):
        rank[s] = count
        return count + (high[s] >= 0).astype(I32)

    lax.fori_loop(0, total, number, 0)

    def base_of(kind, row, node):
        return ((kind * 2 + row) * zn + node) * steps

    def place(base, t, s, earliest, ok):
        t = jnp.where(ok, jnp.maximum(t, earliest), t)
        sched[base + t] = jnp.where(ok, s, -1)
        return t + ok.astype(I32)

    longest = 0
    for row in range(2):
        for kind in range(2):

            def node_body(i, carry, row=row, kind=kind):
                longest, before = carry
                node = i if kind == 0 else zn - 1 - i
                base = base_of(kind, row, node)

                def beyond(s):
                    return high[s] > node if kind == 0 else low[s] < node

                def own(j, t):
                    s = (2 * node + row) * per_chip + j
                    return place(base, t, s, 0, beyond(s))

                t = lax.fori_loop(0, per_chip, own, 0)
                last = jnp.clip(node - 1 if kind == 0 else node + 1, 0, zn - 1)

                def pass_on(k, t):
                    s = sched[base_of(kind, row, last) + k]
                    known = jnp.maximum(s, 0)
                    return place(base, t, s, k + 1, (s >= 0) & beyond(known))

                t = lax.fori_loop(0, before, pass_on, t)
                cnt[(kind * 2 + row) * zn + node] = t
                return jnp.maximum(longest, t), t

            longest, _ = lax.fori_loop(0, zn, node_body, (longest, 0))

    for row in range(2):

        def cross_body(z, longest, row=row):
            base = base_of(2, row, z)
            other = 2 * z + 1 - row

            def own(j, t):
                s = (2 * z + row) * per_chip + j
                return place(base, t, s, 0, need[other * total + s] > 0)

            t = lax.fori_loop(0, per_chip, own, 0)
            left, right = jnp.maximum(z - 1, 0), jnp.minimum(z + 1, zn - 1)
            from_left = jnp.where(z > 0, cnt[row * zn + left], 0)
            from_right = jnp.where(z < zn - 1, cnt[(2 + row) * zn + right], 0)

            def arrive(k, t):
                for kind, node, count in ((0, left, from_left), (1, right, from_right)):
                    s = sched[base_of(kind, row, node) + k]
                    known = jnp.maximum(s, 0)
                    ok = (k < count) & (s >= 0) & (need[other * total + known] > 0)
                    t = place(base, t, s, k + 1, ok)
                return t

            t = lax.fori_loop(0, jnp.maximum(from_left, from_right), arrive, t)
            return jnp.maximum(longest, t)

        longest = lax.fori_loop(0, zn, cross_body, longest)

    chip = 2 * zi + yi

    def slot_of(s):
        return jnp.where(s < 0, plan.trash, per_chip + rank[jnp.maximum(s, 0)])

    def place_of(s):
        j = s - chip * per_chip
        mine = (j >= 0) & (j < per_chip)
        half = (j // plan.owned != ci).astype(I32)
        return jnp.where(mine, half * plan.owned + lax.rem(jnp.maximum(j, 0), plan.owned), slot_of(s))

    left, right = jnp.maximum(zi - 1, 0), jnp.minimum(zi + 1, zn - 1)

    def write(k):
        out[k] = place_of(sched[base_of(0, 0, 0) + yi * zn * steps + zi * steps + k])
        out[steps + k] = place_of(sched[base_of(1, 0, 0) + yi * zn * steps + zi * steps + k])
        out[2 * steps + k] = place_of(sched[base_of(2, 0, 0) + yi * zn * steps + zi * steps + k])
        s = sched[base_of(0, 0, 0) + yi * zn * steps + left * steps + k]
        out[3 * steps + k] = slot_of(jnp.where(zi > 0, s, -1))
        s = sched[base_of(1, 0, 0) + yi * zn * steps + right * steps + k]
        out[4 * steps + k] = slot_of(jnp.where(zi < zn - 1, s, -1))
        out[5 * steps + k] = slot_of(sched[base_of(2, 0, 0) + (1 - yi) * zn * steps + zi * steps + k])

    each(steps, write)
    for b in range(FMAX):
        out[plan.own_at + b] = place_of(stored[(2 * chip + ci) * FMAX + b])
        out[plan.partner_at + b] = place_of(stored[(2 * chip + 1 - ci) * FMAX + b])
    out[plan.rounds_at] = longest


def make_tables(plan, start, adapter, home, me):
    smem = pl.BlockSpec(memory_space=pltpu.SMEM)
    return pl.pallas_call(
        functools.partial(table_kernel, plan),
        out_shape=jax.ShapeDtypeStruct((plan.size,), I32),
        in_specs=[smem] * 4,
        out_specs=smem,
        scratch_shapes=[
            pltpu.SMEM((plan.blocks,), I32),
            pltpu.SMEM((2 * plan.zn * plan.adapters,), I32),
            pltpu.SMEM((plan.adapters,), I32),
            pltpu.SMEM((plan.adapters,), I32),
            pltpu.SMEM((plan.adapters,), I32),
            pltpu.SMEM((6 * plan.zn * plan.steps,), I32),
            pltpu.SMEM((4 * plan.zn,), I32),
        ],
    )(start, adapter, home, me)


def fill_kernel(owned, kept, got, out):
    @pl.when(pl.program_id(0) < owned)
    def _():
        out[...] = kept[...]

    @pl.when(pl.program_id(0) >= owned)
    def _():
        out[...] = got[...]


def fill_store(plan, kept, got):
    owned = plan.owned
    block = (1, *kept.shape[1:])
    return pl.pallas_call(
        functools.partial(fill_kernel, owned),
        out_shape=jax.ShapeDtypeStruct((plan.slots, *kept.shape[1:]), kept.dtype),
        grid=(2 * owned,),
        in_specs=[
            pl.BlockSpec(block, lambda i: (jnp.minimum(i, owned - 1), 0, 0)),
            pl.BlockSpec(block, lambda i: (jnp.maximum(i - owned, 0), 0, 0)),
        ],
        out_specs=pl.BlockSpec(block, lambda i: (i, 0, 0)),
    )(kept, got)


def base_kernel(count, depth, order, tok, *refs):
    pieces, out = refs[:count], refs[count]
    lhs = [tok[:, pl.ds(pl.multiple_of(order[i] * depth, LANES), depth)] for i in range(count)]
    out[...] = jnp.dot(
        jnp.concatenate(lhs, axis=1),
        jnp.concatenate([p[...] for p in pieces], axis=0),
        preferred_element_type=F32,
    ).astype(out.dtype)


def base_product(tokens, pieces, order, dtype, block_rows):
    rows, width = tokens.shape
    depth, cols = pieces[0].shape
    return pl.pallas_call(
        functools.partial(base_kernel, len(pieces), depth),
        out_shape=jax.ShapeDtypeStruct((rows, cols), dtype),
        grid_spec=pltpu.PrefetchScalarGridSpec(
            num_scalar_prefetch=1,
            grid=(rows // block_rows,),
            in_specs=[pl.BlockSpec((block_rows, width), lambda i, o: (i, 0))]
            + [pl.BlockSpec((depth, cols), lambda i, o: (0, 0))] * len(pieces),
            out_specs=pl.BlockSpec((block_rows, cols), lambda i, o: (i, 0)),
        ),
        cost_estimate=pl.CostEstimate(
            flops=2 * rows * width * cols,
            bytes_accessed=2 * (rows * width + width * cols + rows * cols),
            transcendentals=0,
        ),
    )(order, tokens, *pieces)


def rank_kernel(half, where, tok, own, got, out):
    for j, panel in enumerate((own, got)):
        core = where[0] if j == 0 else 1 - where[0]
        first = pl.multiple_of(core * half, LANES)
        part = jnp.dot(tok[:, pl.ds(first, half)], panel[0], preferred_element_type=F32)
        if j == 0:
            out[...] = part
        else:
            out[...] += part


def rank_product(tokens, store, got, where, half, block_rows):
    rows, width = tokens.shape
    lanes = store.shape[2]
    return pl.pallas_call(
        functools.partial(rank_kernel, half),
        out_shape=jax.ShapeDtypeStruct((rows, lanes), F32),
        grid_spec=pltpu.PrefetchScalarGridSpec(
            num_scalar_prefetch=1,
            grid=(rows // block_rows,),
            in_specs=[
                pl.BlockSpec((block_rows, width), lambda b, w: (b, 0)),
                pl.BlockSpec((1, half, lanes), lambda b, w: (w[1 + b], 0, 0)),
                pl.BlockSpec((1, half, lanes), lambda b, w: (b, 0, 0)),
            ],
            out_specs=pl.BlockSpec((block_rows, lanes), lambda b, w: (b, 0)),
        ),
        cost_estimate=pl.CostEstimate(
            flops=2 * rows * width * lanes, bytes_accessed=2 * rows * width + 4 * rows * lanes, transcendentals=0
        ),
    )(where, tokens, store, got)


def final_kernel(others, up_rank, where, rank, base, *refs):
    rank_got, base_got = refs[:others], refs[others : 2 * others]
    panels, out, up = refs[2 * others : 2 * others + 2], refs[2 * others + 2], refs[2 * others + 3]
    full = rank[...]
    value = base[...]
    for j in range(others):
        full += rank_got[j][...].astype(F32)
        value += base_got[j][...].astype(F32)
    for j in range(2):
        core = where[0] if j == 0 else 1 - where[0]
        first = pl.multiple_of(core * up_rank, up_rank)
        for c in range(out.shape[1] // LANES):
            up[pl.ds(first, up_rank), c * LANES : (c + 1) * LANES] = panels[j][0, c * up_rank : (c + 1) * up_rank, :]
    delta = jnp.dot(full.astype(BF), up[...], preferred_element_type=F32)
    out[...] = (value + adapter_scale * delta).astype(out.dtype)


def final_sum(rank, rank_got, base, base_got, store, got, where, half, block_rows):
    rows, cols = base.shape
    rank_width = rank.shape[1]
    up_rank = rank_width // 2
    up_rows = store.shape[1] - half
    others = len(rank_got)
    row_block = pl.BlockSpec((block_rows, rank_width), lambda b, w: (b, 0))
    value_block = pl.BlockSpec((block_rows, cols), lambda b, w: (b, 0))
    return pl.pallas_call(
        functools.partial(final_kernel, others, up_rank),
        out_shape=jax.ShapeDtypeStruct((rows, cols), BF),
        grid_spec=pltpu.PrefetchScalarGridSpec(
            num_scalar_prefetch=1,
            grid=(rows // block_rows,),
            in_specs=[row_block, value_block]
            + [row_block] * others
            + [value_block] * others
            + [
                pl.BlockSpec((1, up_rows, LANES), lambda b, w: (w[1 + b], half // up_rows, 0)),
                pl.BlockSpec((1, up_rows, LANES), lambda b, w: (b, half // up_rows, 0)),
            ],
            out_specs=value_block,
            scratch_shapes=[pltpu.VMEM((rank_width, cols), BF)],
        ),
        cost_estimate=pl.CostEstimate(
            flops=2 * rows * rank_width * cols, bytes_accessed=8 * rows * cols, transcendentals=0
        ),
    )(where, rank, base, *rank_got, *base_got, store, got)


def body(tokens, value_weight, adapter_down, adapter_up, req_start, req_adapter, adapter_home):
    rows, width = tokens.shape
    tp = lax.axis_size("tp")
    zn = lax.axis_size("z")
    owned, _, rank_width = adapter_down.shape
    depth = value_weight.shape[0]
    cols = adapter_up.shape[2]
    block_rows = rows // FMAX
    half = width // 2
    zi, yi, ci, ti = (lax.axis_index(a).astype(I32) for a in ("z", "y", "c", "tp"))
    plan = Plan(zn, owned, req_start.shape[0], block_rows)
    thin = depth % LANES != 0

    down = adapter_down.reshape(owned, 2, half, rank_width)
    up = adapter_up.reshape(owned, 2, rank_width // 2, cols // LANES, LANES).transpose(0, 1, 3, 2, 4)
    both = jnp.concatenate([down, up.reshape(owned, 2, -1, LANES)], axis=2)
    kept = lax.dynamic_index_in_dim(both, ci, 1, keepdims=False)
    given = lax.dynamic_index_in_dim(both, 1 - ci, 1, keepdims=False)
    store = fill_store(plan, kept, swap(given, "c"))

    early = []
    if not thin:
        parts = [
            lax.dynamic_slice_in_dim(value_weight, lax.rem(ti + shift, tp) * cols, cols, 1)
            for shift in list(range(1, tp)) + [0]
        ]
        early = [[p] + [rotate(p, "z", s) for s in range(1, zn)] for p in parts[:-1]]
        early_y = [[swap(p, "y")] for p in parts]
        late = parts[-1]

    table = make_tables(plan, req_start, req_adapter, adapter_home, jnp.stack([zi, yi, ci]))

    zs = [lax.rem(zi - s + zn, zn) for s in range(zn)]
    order = jnp.stack(
        [z * 4 + y * 2 + c for c in (ci, 1 - ci) for y in (yi, 1 - yi) for z in zs]
    )

    def one_round(k, store):
        pick = lambda at: lax.dynamic_index_in_dim(store, at, 0, keepdims=False)
        steps = plan.steps
        at = [lax.dynamic_index_in_dim(table, i * steps + k, 0, keepdims=False) for i in range(6)]
        moved = [
            step_z(pick(at[0]), 0),
            step_z(pick(at[1]), 1),
            swap(pick(at[2]), "y"),
        ]
        for i in range(3):
            store = lax.dynamic_update_index_in_dim(store, moved[i], at[3 + i], 0)
        return store

    def spread(along_z, along_y):
        pieces = along_z + along_y
        return pieces + [swap(p, "c") for p in pieces]

    def run(unrolled, loop, table, store, tokens, value_weight, *rest):
        for k in range(unrolled):
            store = one_round(k, store)
        if loop:
            rounds = jnp.maximum(table[plan.rounds_at], unrolled)
            store = lax.fori_loop(unrolled, rounds, one_round, store)

        if thin:
            full = lax.all_gather(value_weight, ("z", "y", "c"), axis=0, tiled=True)
            product = jnp.dot(tokens, full, preferred_element_type=F32)
            base = lax.psum_scatter(product.astype(BF), "tp", scatter_dimension=1, tiled=True).astype(F32)
            base_got = []
        else:
            early, early_y, late = rest
            base_got = []
            for i, along_z in enumerate(early):
                along_y = early_y[i] + [swap(p, "y") for p in along_z[1:]]
                part = base_product(tokens, spread(along_z, along_y), order, BF, block_rows)
                base_got.append(rotate(part, "tp", i + 1))
            along_z = [late] + [rotate(late, "z", s) for s in range(1, zn)]
            along_y = early_y[-1] + [swap(p, "y") for p in along_z[1:]]
            base = base_product(tokens, spread(along_z, along_y), order, F32, block_rows)

        theirs = jnp.take(store, table[plan.partner_at : plan.partner_at + FMAX], axis=0)
        got = swap(theirs, "c")
        where = jnp.concatenate([ci[None], table[plan.own_at : plan.own_at + FMAX]])
        rank = rank_product(tokens, store, got, where, half, block_rows)
        rank_got = [rotate(rank.astype(BF), "tp", s) for s in range(1, tp)]
        if thin:
            base_got = [jnp.zeros(base.shape, BF)] * (tp - 1)
        return final_sum(rank, rank_got, base, base_got, store, got, where, half, block_rows)

    rest = () if thin else (early, early_y, late)
    rounds = table[plan.rounds_at]
    tiers = [(n, False) for n in UNROLLED] + [(UNROLLED[0], True)]
    tier = sum((rounds > n).astype(I32) for n in UNROLLED)
    return lax.switch(
        tier,
        [functools.partial(run, n, loop) for n, loop in tiers],
        table, store, tokens, value_weight, *rest,
    )


def solution(mesh):
    tp, ad = mesh.shape["tp"], mesh.shape["ad"]
    fine = Mesh(mesh.devices.reshape(tp, ad // 4, 2, 2), ("tp", "z", "y", "c"))
    at = ("z", "y", "c")
    return jax.shard_map(
        body,
        mesh=fine,
        in_specs=(
            P(at, "tp"),
            P(("tp",) + at, None),
            P(at, "tp", None),
            P(at, None, "tp"),
            P(),
            P(),
            P(),
        ),
        out_specs=P(at, "tp"),
        check_vma=False,
    )
```

```python
import functools

import jax
import jax.numpy as jnp
from jax import lax
from jax.experimental import pallas as pl
from jax.experimental.pallas import tpu as pltpu
from jax.sharding import Mesh
from jax.sharding import PartitionSpec as P

FMAX = 4
LANES = 128
PAIR = 2
CHIP = 5

adapter_scale = 2.0
BF = jnp.bfloat16
F32 = jnp.float32
I32 = jnp.int32


def swap(array, axis):
    return lax.ppermute(array, axis, [(0, 1), (1, 0)])


def rotate(array, axis, shift):
    count = lax.axis_size(axis)
    return lax.ppermute(array, axis, [(i, (i + shift) % count) for i in range(count)])


def together(*groups):
    flat = lax.optimization_barrier(tuple(x for g in groups for x in g))
    out, at = [], 0
    for g in groups:
        out.append(list(flat[at : at + len(g)]))
        at += len(g)
    return out


class Plan:
    def __init__(self, zn, owned, requests, block_rows):
        self.zn, self.owned, self.requests, self.block_rows = zn, owned, requests, block_rows
        self.here = 4 * owned
        self.adapters = zn * self.here
        self.blocks = zn * 4 * FMAX
        self.most_chip = min(2 * FMAX, self.adapters)
        self.send_at = 0
        self.mine_at = self.send_at + (zn - 1) * self.here
        self.partner_at = self.mine_at + self.most_chip
        self.slot_at = self.partner_at + self.most_chip
        self.pair_at = self.slot_at + FMAX
        self.chip_at = self.pair_at + zn
        self.trash = self.chip_at + 1
        self.size = self.trash + 1


def table_kernel(plan, start, adapter, home, me, out, stored, chip_need, z_need, pairs, loc, pos, counts):
    zn, here, owned, total = plan.zn, plan.here, plan.owned, plan.adapters
    zi, yi, ci = me[0], me[1], me[2]
    unroll = 8

    def clear(ref, count):
        def some(i, c):
            for j in range(unroll):
                ref[i * unroll + j] = 0
            return c

        lax.fori_loop(0, count // unroll, some, 0)
        for j in range(count - count % unroll, count):
            ref[j] = 0

    clear(chip_need, 2 * zn * total)
    clear(z_need, zn * total)
    clear(pairs, zn * zn)
    clear(counts, 2 * zn)
    clear(out, plan.size)

    def block(b, r):
        following = jnp.minimum(r + 1, plan.requests - 1)
        r = jnp.where((r + 1 < plan.requests) & (start[following] <= b * plan.block_rows), r + 1, r)
        s = home[adapter[r]]
        stored[b] = s
        chip = b // (2 * FMAX)
        at = chip * total + s
        counts[chip] = counts[chip] + 1 - chip_need[at]
        chip_need[at] = 1
        z_need[(b // (4 * FMAX)) * total + s] = 1
        out[plan.chip_at] = jnp.maximum(out[plan.chip_at], counts[chip])
        return r

    lax.fori_loop(0, plan.blocks, block, 0)

    def relative(s):
        local = lax.rem(s, here)
        device = local // owned
        y, c = device // 2, lax.rem(device, 2)
        arm = (y != yi).astype(I32) + 2 * (c != ci).astype(I32)
        return arm * owned + lax.rem(local, owned)

    def place(shift, k):
        early = here + (shift - 1) * PAIR + k
        late = here + (zn - 1) * PAIR + (shift - 1) * (here - PAIR) + k - PAIR
        return jnp.where(k < PAIR, early, late)

    def source(zs, carry):
        def one(j, carry):
            s = zs * here + j

            def target(zd, carry):
                used = z_need[zd * total + s]
                k = pairs[zs * zn + zd]
                pairs[zs * zn + zd] = k + used
                shift = lax.rem(zd - zs + zn, zn)
                far = (used > 0) & (shift > 0)
                at = jnp.where(far & (zs == zi), plan.send_at + (shift - 1) * here + k, plan.trash)
                out[at] = relative(s)
                out[plan.pair_at + shift] = jnp.maximum(out[plan.pair_at + shift], jnp.where(far, k + 1, 0))
                return carry

            arrived = pairs[zs * zn + zi]
            shift = lax.rem(zi - zs + zn, zn)
            loc[s] = jnp.where(zs == zi, relative(s), place(shift, arrived))
            return lax.fori_loop(0, zn, target, carry)

        return lax.fori_loop(0, here, one, carry)

    lax.fori_loop(0, zn, source, 0)

    chip = 2 * zi + yi
    other = 2 * zi + 1 - yi

    def enlist(s, carry):
        mine, theirs = carry
        use_mine, use_theirs = chip_need[chip * total + s], chip_need[other * total + s]
        out[jnp.where(use_mine > 0, plan.mine_at + mine, plan.trash)] = loc[s]
        pos[s] = mine
        out[jnp.where(use_theirs > 0, plan.partner_at + theirs, plan.trash)] = loc[s]
        return mine + use_mine, theirs + use_theirs

    lax.fori_loop(0, total, enlist, (0, 0))
    for b in range(FMAX):
        out[plan.slot_at + b] = pos[stored[(2 * chip + ci) * FMAX + b]]


def make_tables(plan, start, adapter, home, me):
    smem = pl.BlockSpec(memory_space=pltpu.SMEM)
    return pl.pallas_call(
        functools.partial(table_kernel, plan),
        out_shape=jax.ShapeDtypeStruct((plan.size,), I32),
        in_specs=[smem] * 4,
        out_specs=smem,
        scratch_shapes=[
            pltpu.SMEM((plan.blocks,), I32),
            pltpu.SMEM((2 * plan.zn * plan.adapters,), I32),
            pltpu.SMEM((plan.zn * plan.adapters,), I32),
            pltpu.SMEM((plan.zn * plan.zn,), I32),
            pltpu.SMEM((plan.adapters,), I32),
            pltpu.SMEM((plan.adapters,), I32),
            pltpu.SMEM((2 * plan.zn,), I32),
        ],
    )(start, adapter, home, me)


def pick_kernel(counts, groups, table, step, *refs):
    sources, outs, sem = refs[: len(counts)], refs[len(counts) : -1], refs[-1]
    taken = []
    for g, group in enumerate(groups):
        for i, at in enumerate(group):
            index = table[at + step[0]]
            first = 0
            for r, count in enumerate(counts):
                here = jnp.clip(index - first, 0, count - 1)
                copy = pltpu.make_async_copy(sources[r].at[here], outs[g].at[i], sem.at[len(taken)])
                pl.when((index >= first) & (index < first + count))(copy.start)
                first += count
            taken.append(pltpu.make_async_copy(sources[0].at[0], outs[g].at[i], sem.at[len(taken)]))
    for copy in taken:
        copy.wait()


def pick(table, sources, groups, step=0):
    panel = sources[0].shape[1:]
    many = sum(len(g) for g in groups)
    size = 2 * panel[0] * panel[1]
    return pl.pallas_call(
        functools.partial(pick_kernel, tuple(s.shape[0] for s in sources), tuple(tuple(g) for g in groups)),
        out_shape=[jax.ShapeDtypeStruct((len(g), *panel), BF) for g in groups],
        grid_spec=pltpu.PrefetchScalarGridSpec(
            num_scalar_prefetch=2,
            grid=(1,),
            in_specs=[pl.BlockSpec(memory_space=pl.ANY)] * len(sources),
            out_specs=[pl.BlockSpec(memory_space=pltpu.VMEM)] * len(groups),
            scratch_shapes=[pltpu.SemaphoreType.DMA((many,))],
        ),
        cost_estimate=pl.CostEstimate(flops=0, bytes_accessed=2 * size * many, transcendentals=0),
    )(table, jnp.asarray(step, I32).reshape(1), *sources)


def blank(shape):
    return pl.pallas_call(
        lambda out: None,
        out_shape=jax.ShapeDtypeStruct(shape, BF),
        out_specs=pl.BlockSpec(memory_space=pl.ANY),
    )()


def base_kernel(count, depth, order, tok, *refs):
    pieces, out = refs[:count], refs[count]
    lhs = [tok[:, pl.ds(pl.multiple_of(order[i] * depth, LANES), depth)] for i in range(count)]
    out[...] = jnp.dot(
        jnp.concatenate(lhs, axis=1),
        jnp.concatenate([p[...] for p in pieces], axis=0),
        preferred_element_type=F32,
    ).astype(out.dtype)


def base_product(tokens, pieces, order, cols, dtype, block_rows):
    rows, width = tokens.shape
    depth = pieces[0].shape[0]
    count = len(pieces)
    return pl.pallas_call(
        functools.partial(base_kernel, count, depth),
        out_shape=jax.ShapeDtypeStruct((rows, cols), dtype),
        grid_spec=pltpu.PrefetchScalarGridSpec(
            num_scalar_prefetch=1,
            grid=(rows // block_rows,),
            in_specs=[pl.BlockSpec((block_rows, width), lambda i, o: (i, 0))]
            + [pl.BlockSpec((depth, cols), lambda i, o: (0, o[count]))] * count,
            out_specs=pl.BlockSpec((block_rows, cols), lambda i, o: (i, 0)),
        ),
        cost_estimate=pl.CostEstimate(
            flops=2 * rows * width * cols,
            bytes_accessed=2 * (rows * width + width * cols + rows * cols),
            transcendentals=0,
        ),
    )(order, tokens, *pieces)


def chosen(main, spare, slot):
    return jnp.where(slot < CHIP, main, spare)


def rank_kernel(have, where, *refs):
    toks, mains, spares = refs[:2], refs[2:4], refs[4:6]
    outs = refs[6 + have :]
    slot = where[2 + pl.program_id(0)]
    total = refs[6][...] if have else None
    for tok, main, spare in zip(toks, mains, spares):
        part = jnp.dot(tok[...], chosen(main[0], spare[0], slot), preferred_element_type=F32)
        total = part if total is None else total + part
    outs[0][...] = total
    if have:
        outs[1][...] = total.astype(BF)


def main_slot(s):
    return jnp.minimum(s, CHIP - 1)


def spare_slot(s):
    return jnp.maximum(s - CHIP, 0)


def rank_product(tokens, mains, spares, where, before, quarter, block_rows):
    rows, width = tokens.shape
    lanes = mains[0].shape[2]
    have = before is not None
    result = pl.BlockSpec((block_rows, lanes), lambda b, w: (b, 0))
    return pl.pallas_call(
        functools.partial(rank_kernel, int(have)),
        out_shape=[jax.ShapeDtypeStruct((rows, lanes), t) for t in ([F32, BF] if have else [F32])],
        grid_spec=pltpu.PrefetchScalarGridSpec(
            num_scalar_prefetch=1,
            grid=(rows // block_rows,),
            in_specs=[pl.BlockSpec((block_rows, quarter), lambda b, w, i=i: (b, w[i])) for i in range(2)]
            + [pl.BlockSpec((1, quarter, lanes), lambda b, w: (main_slot(w[2 + b]), 0, 0))] * 2
            + [pl.BlockSpec((1, quarter, lanes), lambda b, w: (spare_slot(w[2 + b]), 0, 0))] * 2
            + [result] * have,
            out_specs=[result] * (1 + have),
        ),
        cost_estimate=pl.CostEstimate(
            flops=rows * width * lanes, bytes_accessed=rows * width + 8 * rows * lanes, transcendentals=0
        ),
    )(where, tokens, tokens, *mains, *spares, *([before] if have else []))


def final_kernel(others, up_rank, where, rank, base, *refs):
    rank_got, base_got = refs[:others], refs[others : 2 * others]
    mains, spares = refs[2 * others : 2 * others + 4], refs[2 * others + 4 : 2 * others + 8]
    out, up = refs[-2], refs[-1]
    slot = where[4 + pl.program_id(0)]
    full = rank[...]
    value = base[...]
    for j in range(others):
        full += rank_got[j][...].astype(F32)
        value += base_got[j][...].astype(F32)
    for g in range(4):
        first = pl.multiple_of(where[g] * up_rank, up_rank)
        panel = chosen(mains[g][0], spares[g][0], slot)
        for c in range(out.shape[1] // LANES):
            up[pl.ds(first, up_rank), c * LANES : (c + 1) * LANES] = panel[c * up_rank : (c + 1) * up_rank, :]
    delta = jnp.dot(full.astype(BF), up[...], preferred_element_type=F32)
    out[...] = (value + adapter_scale * delta).astype(out.dtype)


def final_sum(rank, rank_got, base, base_got, mains, spares, where, quarter, block_rows):
    rows, cols = base.shape
    rank_width = rank.shape[1]
    up_rank = rank_width // 4
    up_rows = mains[0].shape[1] - quarter
    at = quarter // up_rows
    others = len(rank_got)
    row_block = pl.BlockSpec((block_rows, rank_width), lambda b, w: (b, 0))
    value_block = pl.BlockSpec((block_rows, cols), lambda b, w: (b, 0))
    return pl.pallas_call(
        functools.partial(final_kernel, others, up_rank),
        out_shape=jax.ShapeDtypeStruct((rows, cols), BF),
        grid_spec=pltpu.PrefetchScalarGridSpec(
            num_scalar_prefetch=1,
            grid=(rows // block_rows,),
            in_specs=[row_block, value_block]
            + [row_block] * others
            + [value_block] * others
            + [pl.BlockSpec((1, up_rows, LANES), lambda b, w: (main_slot(w[4 + b]), at, 0))] * 4
            + [pl.BlockSpec((1, up_rows, LANES), lambda b, w: (spare_slot(w[4 + b]), at, 0))] * 4,
            out_specs=value_block,
            scratch_shapes=[pltpu.VMEM((rank_width, cols), BF)],
        ),
        cost_estimate=pl.CostEstimate(
            flops=2 * rows * rank_width * cols, bytes_accessed=8 * rows * cols, transcendentals=0
        ),
    )(where, rank, base, *rank_got, *base_got, *mains, *spares)


def body(tokens, value_weight, adapter_down, adapter_up, req_start, req_adapter, adapter_home):
    rows, width = tokens.shape
    tp = lax.axis_size("tp")
    zn = lax.axis_size("z")
    owned, _, rank_width = adapter_down.shape
    depth = value_weight.shape[0]
    cols = adapter_up.shape[2]
    block_rows = rows // FMAX
    quarter = width // 4
    zi, yi, ci, ti = (lax.axis_index(a).astype(I32) for a in ("z", "y", "c", "tp"))
    plan = Plan(zn, owned, req_start.shape[0], block_rows)
    here = plan.here
    thin = depth % LANES != 0
    table = make_tables(plan, req_start, req_adapter, adapter_home, jnp.stack([zi, yi, ci]))

    down = adapter_down.reshape(owned, 4, quarter, rank_width)
    up = adapter_up.reshape(owned, 4, rank_width // 4, cols // LANES, LANES).transpose(0, 1, 3, 2, 4)
    slab = jnp.concatenate([down, up.reshape(owned, 4, -1, LANES)], axis=2).transpose(1, 0, 2, 3)
    order_y = [yi, 1 - yi, yi, 1 - yi]
    order_c = [ci, ci, 1 - ci, 1 - ci]
    quarters = [y * 2 + c for y, c in zip(order_y, order_c)]
    part = [lax.dynamic_index_in_dim(slab, q, 0, keepdims=False) for q in quarters]
    diagonal = [(0, 3), (1, 2), (2, 1), (3, 0)]
    local = [part[0], swap(part[1], "y"), swap(part[2], "c"), lax.ppermute(part[3], ("y", "c"), diagonal)]

    shifts = sorted(range(1, zn), key=lambda s: -min(s, zn - s))
    if not thin:
        along_z = [value_weight] + [rotate(value_weight, "z", s) for s in shifts]

    def send_at(shift):
        return plan.send_at + (shift - 1) * here

    pays = pick(table, local, [[send_at(s) + k for k in range(PAIR)] for s in range(1, zn)])
    got = [rotate(p, "z", s) for s, p in zip(range(1, zn), pays)]

    if not thin:
        along_y = [swap(p, "y") for p in along_z]
        got, along_z, along_y = together(got, along_z, along_y)

    spare = blank(((zn - 1) * (here - PAIR), *slab.shape[2:]))
    for s in range(1, zn):

        def extra(k, spare, s=s):
            (pay,) = pick(table, local, [[send_at(s)]], k)
            return lax.dynamic_update_slice_in_dim(spare, rotate(pay, "z", s), (s - 1) * (here - PAIR) + k - PAIR, 0)

        spare = lax.fori_loop(PAIR, jnp.maximum(table[plan.pair_at + s], PAIR), extra, spare)
    sources = local + got + [spare]

    def exchange(first, last):
        mine, theirs = pick(
            table,
            sources,
            [[plan.mine_at + j for j in range(first, last)], [plan.partner_at + j for j in range(first, last)]],
        )
        crossed = swap(theirs, "y")
        return [mine, crossed, swap(mine, "c"), swap(crossed, "c")]

    mains = exchange(0, CHIP)
    more = (plan.most_chip - CHIP, *slab.shape[2:])
    spares = lax.cond(
        table[plan.chip_at] > CHIP,
        lambda: exchange(CHIP, plan.most_chip),
        lambda: [blank(more) for _ in range(4)],
    )

    if thin:
        full = lax.all_gather(value_weight, ("z", "y", "c"), axis=0, tiled=True)
        product = jnp.dot(tokens, full, preferred_element_type=F32)
        base = lax.psum_scatter(product.astype(BF), "tp", scatter_dimension=1, tiled=True).astype(F32)
        base_got = [jnp.zeros(base.shape, BF)] * (tp - 1)
    else:
        pieces = along_z + along_y
        pieces = pieces + [swap(p, "c") for p in pieces]
        places = [
            lax.rem(zi - s + zn, zn) * 4 + q for q in quarters for s in [0] + shifts
        ]
        base_got = []
        for shift in range(1, tp):
            order = jnp.stack(places + [lax.rem(ti + shift, tp)])
            base_got.append(rotate(base_product(tokens, pieces, order, cols, BF, block_rows), "tp", shift))
        base = base_product(tokens, pieces, jnp.stack(places + [ti]), cols, F32, block_rows)

    slot = table[plan.slot_at : plan.slot_at + FMAX]
    where = [jnp.concatenate([jnp.stack([quarters[i], quarters[i + 2]]), slot]) for i in range(2)]
    (rank,) = rank_product(tokens, mains[0::2], spares[0::2], where[0], None, quarter, block_rows)
    rank, rank_bf = rank_product(tokens, mains[1::2], spares[1::2], where[1], rank, quarter, block_rows)
    rank_got = [rotate(rank_bf, "tp", s) for s in range(1, tp)]
    where = jnp.concatenate([jnp.stack(quarters), slot])
    return final_sum(rank, rank_got, base, base_got, mains, spares, where, quarter, block_rows)


def solution(mesh):
    tp, ad = mesh.shape["tp"], mesh.shape["ad"]
    fine = Mesh(mesh.devices.reshape(tp, ad // 4, 2, 2), ("tp", "z", "y", "c"))
    at = ("z", "y", "c")
    return jax.shard_map(
        body,
        mesh=fine,
        in_specs=(
            P(at, "tp"),
            P(("tp",) + at, None),
            P(at, "tp", None),
            P(at, None, "tp"),
            P(),
            P(),
            P(),
        ),
        out_specs=P(at, "tp"),
        check_vma=False,
    )
```

```python
import functools

import jax
import jax.numpy as jnp
from jax import lax
from jax.experimental import pallas as pl
from jax.experimental.pallas import tpu as pltpu
from jax.sharding import Mesh
from jax.sharding import PartitionSpec as P


FMAX = 4
LANES = 128
PAIR = 2
CHIP = 5

adapter_scale = 2.0
BF = jnp.bfloat16
F32 = jnp.float32
I32 = jnp.int32


def swap(array, axis):
    return lax.ppermute(array, axis, [(0, 1), (1, 0)])


def rotate(array, axis, shift):
    count = lax.axis_size(axis)
    return lax.ppermute(array, axis, [(i, (i + shift) % count) for i in range(count)])


def together(*groups):
    flat = lax.optimization_barrier(tuple(x for g in groups for x in g))
    out, at = [], 0
    for g in groups:
        out.append(list(flat[at : at + len(g)]))
        at += len(g)
    return out


class Plan:
    def __init__(self, zn, owned, requests, block_rows):
        self.zn, self.owned, self.requests, self.block_rows = zn, owned, requests, block_rows
        self.here = 4 * owned
        self.adapters = zn * self.here
        self.blocks = zn * 4 * FMAX
        self.most_chip = min(2 * FMAX, self.adapters)
        self.send_at = 0
        self.mine_at = self.send_at + (zn - 1) * self.here
        self.partner_at = self.mine_at + self.most_chip
        self.slot_at = self.partner_at + self.most_chip
        self.pair_at = self.slot_at + FMAX
        self.chip_at = self.pair_at + zn
        self.trash = self.chip_at + 1
        self.size = self.trash + 1


def table_kernel(plan, start, adapter, home, me, out, stored, chip_need, z_need, pairs, loc, pos, counts):
    zn, here, owned, total = plan.zn, plan.here, plan.owned, plan.adapters
    zi, yi, ci = me[0], me[1], me[2]
    unroll = 8

    def clear(ref, count):
        def some(i, c):
            for j in range(unroll):
                ref[i * unroll + j] = 0
            return c

        lax.fori_loop(0, count // unroll, some, 0)
        for j in range(count - count % unroll, count):
            ref[j] = 0

    clear(chip_need, 2 * zn * total)
    clear(z_need, zn * total)
    clear(pairs, zn * zn)
    clear(counts, 2 * zn)
    clear(out, plan.size)

    def block(b, r):
        following = jnp.minimum(r + 1, plan.requests - 1)
        r = jnp.where((r + 1 < plan.requests) & (start[following] <= b * plan.block_rows), r + 1, r)
        s = home[adapter[r]]
        stored[b] = s
        chip = b // (2 * FMAX)
        at = chip * total + s
        counts[chip] = counts[chip] + 1 - chip_need[at]
        chip_need[at] = 1
        z_need[(b // (4 * FMAX)) * total + s] = 1
        out[plan.chip_at] = jnp.maximum(out[plan.chip_at], counts[chip])
        return r

    lax.fori_loop(0, plan.blocks, block, 0)

    def relative(s):
        local = lax.rem(s, here)
        device = local // owned
        y, c = device // 2, lax.rem(device, 2)
        arm = (y != yi).astype(I32) + 2 * (c != ci).astype(I32)
        return arm * owned + lax.rem(local, owned)

    def place(shift, k):
        early = here + (shift - 1) * PAIR + k
        late = here + (zn - 1) * PAIR + (shift - 1) * (here - PAIR) + k - PAIR
        return jnp.where(k < PAIR, early, late)

    def source(zs, carry):
        def one(j, carry):
            s = zs * here + j

            def target(zd, carry):
                used = z_need[zd * total + s]
                k = pairs[zs * zn + zd]
                pairs[zs * zn + zd] = k + used
                shift = lax.rem(zd - zs + zn, zn)
                far = (used > 0) & (shift > 0)
                at = jnp.where(far & (zs == zi), plan.send_at + (shift - 1) * here + k, plan.trash)
                out[at] = relative(s)
                out[plan.pair_at + shift] = jnp.maximum(out[plan.pair_at + shift], jnp.where(far, k + 1, 0))
                return carry

            arrived = pairs[zs * zn + zi]
            shift = lax.rem(zi - zs + zn, zn)
            loc[s] = jnp.where(zs == zi, relative(s), place(shift, arrived))
            return lax.fori_loop(0, zn, target, carry)

        return lax.fori_loop(0, here, one, carry)

    lax.fori_loop(0, zn, source, 0)

    chip = 2 * zi + yi
    other = 2 * zi + 1 - yi

    def enlist(s, carry):
        mine, theirs = carry
        use_mine, use_theirs = chip_need[chip * total + s], chip_need[other * total + s]
        out[jnp.where(use_mine > 0, plan.mine_at + mine, plan.trash)] = loc[s]
        pos[s] = mine
        out[jnp.where(use_theirs > 0, plan.partner_at + theirs, plan.trash)] = loc[s]
        return mine + use_mine, theirs + use_theirs

    lax.fori_loop(0, total, enlist, (0, 0))
    for b in range(FMAX):
        out[plan.slot_at + b] = pos[stored[(2 * chip + ci) * FMAX + b]]


def make_tables(plan, start, adapter, home, me):
    smem = pl.BlockSpec(memory_space=pltpu.SMEM)
    return pl.pallas_call(
        functools.partial(table_kernel, plan),
        out_shape=jax.ShapeDtypeStruct((plan.size,), I32),
        in_specs=[smem] * 4,
        out_specs=smem,
        scratch_shapes=[
            pltpu.SMEM((plan.blocks,), I32),
            pltpu.SMEM((2 * plan.zn * plan.adapters,), I32),
            pltpu.SMEM((plan.zn * plan.adapters,), I32),
            pltpu.SMEM((plan.zn * plan.zn,), I32),
            pltpu.SMEM((plan.adapters,), I32),
            pltpu.SMEM((plan.adapters,), I32),
            pltpu.SMEM((2 * plan.zn,), I32),
        ],
    )(start, adapter, home, me)


def pick_kernel(counts, groups, table, step, *refs):
    sources, outs, sem = refs[: len(counts)], refs[len(counts) : -1], refs[-1]
    taken = []
    for g, group in enumerate(groups):
        for i, at in enumerate(group):
            index = table[at + step[0]]
            first = 0
            for r, count in enumerate(counts):
                here = jnp.clip(index - first, 0, count - 1)
                copy = pltpu.make_async_copy(sources[r].at[here], outs[g].at[i], sem.at[len(taken)])
                pl.when((index >= first) & (index < first + count))(copy.start)
                first += count
            taken.append(pltpu.make_async_copy(sources[0].at[0], outs[g].at[i], sem.at[len(taken)]))
    for copy in taken:
        copy.wait()


def pick(table, sources, groups, step=0):
    panel = sources[0].shape[1:]
    many = sum(len(g) for g in groups)
    size = 2 * panel[0] * panel[1]
    return pl.pallas_call(
        functools.partial(pick_kernel, tuple(s.shape[0] for s in sources), tuple(tuple(g) for g in groups)),
        out_shape=[jax.ShapeDtypeStruct((len(g), *panel), BF) for g in groups],
        grid_spec=pltpu.PrefetchScalarGridSpec(
            num_scalar_prefetch=2,
            grid=(1,),
            in_specs=[pl.BlockSpec(memory_space=pl.ANY)] * len(sources),
            out_specs=[pl.BlockSpec(memory_space=pltpu.VMEM)] * len(groups),
            scratch_shapes=[pltpu.SemaphoreType.DMA((many,))],
        ),
        cost_estimate=pl.CostEstimate(flops=0, bytes_accessed=2 * size * many, transcendentals=0),
    )(table, jnp.asarray(step, I32).reshape(1), *sources)


def blank(shape):
    return pl.pallas_call(
        lambda out: None,
        out_shape=jax.ShapeDtypeStruct(shape, BF),
        out_specs=pl.BlockSpec(memory_space=pl.ANY),
    )()


def base_kernel(count, depth, order, tok, *refs):
    pieces, out = refs[:count], refs[count]
    lhs = [tok[:, pl.ds(pl.multiple_of(order[i] * depth, LANES), depth)] for i in range(count)]
    out[...] = jnp.dot(
        jnp.concatenate(lhs, axis=1),
        jnp.concatenate([p[...] for p in pieces], axis=0),
        preferred_element_type=F32,
    ).astype(out.dtype)


def base_product(tokens, pieces, order, cols, dtype, block_rows):
    rows, width = tokens.shape
    depth = pieces[0].shape[0]
    count = len(pieces)
    return pl.pallas_call(
        functools.partial(base_kernel, count, depth),
        out_shape=jax.ShapeDtypeStruct((rows, cols), dtype),
        grid_spec=pltpu.PrefetchScalarGridSpec(
            num_scalar_prefetch=1,
            grid=(rows // block_rows,),
            in_specs=[pl.BlockSpec((block_rows, width), lambda i, o: (i, 0))]
            + [
                pl.BlockSpec((depth, cols), (lambda i, o: (0, 0)) if p.shape[1] == cols else (lambda i, o: (0, o[count])))
                for p in pieces
            ],
            out_specs=pl.BlockSpec((block_rows, cols), lambda i, o: (i, 0)),
        ),
        cost_estimate=pl.CostEstimate(
            flops=2 * rows * width * cols,
            bytes_accessed=2 * (rows * width + width * cols + rows * cols),
            transcendentals=0,
        ),
    )(order, tokens, *pieces)


def chosen(main, spare, slot):
    return jnp.where(slot < CHIP, main, spare)


def rank_kernel(have, where, *refs):
    toks, mains, spares = refs[:2], refs[2:4], refs[4:6]
    outs = refs[6 + have :]
    slot = where[2 + pl.program_id(0)]
    total = refs[6][...] if have else None
    for tok, main, spare in zip(toks, mains, spares):
        part = jnp.dot(tok[...], chosen(main[0], spare[0], slot), preferred_element_type=F32)
        total = part if total is None else total + part
    outs[0][...] = total
    if have:
        outs[1][...] = total.astype(BF)


def main_slot(s):
    return jnp.minimum(s, CHIP - 1)


def spare_slot(s):
    return jnp.maximum(s - CHIP, 0)


def rank_product(tokens, mains, spares, where, before, quarter, block_rows):
    rows, width = tokens.shape
    lanes = mains[0].shape[2]
    have = before is not None
    result = pl.BlockSpec((block_rows, lanes), lambda b, w: (b, 0))
    return pl.pallas_call(
        functools.partial(rank_kernel, int(have)),
        out_shape=[jax.ShapeDtypeStruct((rows, lanes), t) for t in ([F32, BF] if have else [F32])],
        grid_spec=pltpu.PrefetchScalarGridSpec(
            num_scalar_prefetch=1,
            grid=(rows // block_rows,),
            in_specs=[pl.BlockSpec((block_rows, quarter), lambda b, w, i=i: (b, w[i])) for i in range(2)]
            + [pl.BlockSpec((1, quarter, lanes), lambda b, w: (main_slot(w[2 + b]), 0, 0))] * 2
            + [pl.BlockSpec((1, quarter, lanes), lambda b, w: (spare_slot(w[2 + b]), 0, 0))] * 2
            + [result] * have,
            out_specs=[result] * (1 + have),
        ),
        cost_estimate=pl.CostEstimate(
            flops=rows * width * lanes, bytes_accessed=rows * width + 8 * rows * lanes, transcendentals=0
        ),
    )(where, tokens, tokens, *mains, *spares, *([before] if have else []))


def final_kernel(others, up_rank, where, rank, base, *refs):
    rank_got, base_got = refs[:others], refs[others : 2 * others]
    mains, spares = refs[2 * others : 2 * others + 4], refs[2 * others + 4 : 2 * others + 8]
    out, up = refs[-2], refs[-1]
    slot = where[4 + pl.program_id(0)]
    full = rank[...]
    value = base[...]
    for j in range(others):
        full += rank_got[j][...].astype(F32)
        value += base_got[j][...].astype(F32)
    for g in range(4):
        first = pl.multiple_of(where[g] * up_rank, up_rank)
        panel = chosen(mains[g][0], spares[g][0], slot)
        for c in range(out.shape[1] // LANES):
            up[pl.ds(first, up_rank), c * LANES : (c + 1) * LANES] = panel[c * up_rank : (c + 1) * up_rank, :]
    delta = jnp.dot(full.astype(BF), up[...], preferred_element_type=F32)
    out[...] = (value + adapter_scale * delta).astype(out.dtype)


def final_sum(rank, rank_got, base, base_got, mains, spares, where, quarter, block_rows):
    rows, cols = base.shape
    rank_width = rank.shape[1]
    up_rank = rank_width // 4
    up_rows = mains[0].shape[1] - quarter
    at = quarter // up_rows
    others = len(rank_got)
    row_block = pl.BlockSpec((block_rows, rank_width), lambda b, w: (b, 0))
    value_block = pl.BlockSpec((block_rows, cols), lambda b, w: (b, 0))
    return pl.pallas_call(
        functools.partial(final_kernel, others, up_rank),
        out_shape=jax.ShapeDtypeStruct((rows, cols), BF),
        grid_spec=pltpu.PrefetchScalarGridSpec(
            num_scalar_prefetch=1,
            grid=(rows // block_rows,),
            in_specs=[row_block, value_block]
            + [row_block] * others
            + [value_block] * others
            + [pl.BlockSpec((1, up_rows, LANES), lambda b, w: (main_slot(w[4 + b]), at, 0))] * 4
            + [pl.BlockSpec((1, up_rows, LANES), lambda b, w: (spare_slot(w[4 + b]), at, 0))] * 4,
            out_specs=value_block,
            scratch_shapes=[pltpu.VMEM((rank_width, cols), BF)],
        ),
        cost_estimate=pl.CostEstimate(
            flops=2 * rows * rank_width * cols, bytes_accessed=8 * rows * cols, transcendentals=0
        ),
    )(where, rank, base, *rank_got, *base_got, *mains, *spares)


def body(tokens, value_weight, adapter_down, adapter_up, req_start, req_adapter, adapter_home):
    rows, width = tokens.shape
    tp = lax.axis_size("tp")
    zn = lax.axis_size("z")
    owned, _, rank_width = adapter_down.shape
    depth = value_weight.shape[0]
    cols = adapter_up.shape[2]
    block_rows = rows // FMAX
    quarter = width // 4
    zi, yi, ci, ti = (lax.axis_index(a).astype(I32) for a in ("z", "y", "c", "tp"))
    plan = Plan(zn, owned, req_start.shape[0], block_rows)
    here = plan.here
    thin = depth % LANES != 0
    table = make_tables(plan, req_start, req_adapter, adapter_home, jnp.stack([zi, yi, ci]))

    down = adapter_down.reshape(owned, 4, quarter, rank_width)
    up = adapter_up.reshape(owned, 4, rank_width // 4, cols // LANES, LANES).transpose(0, 1, 3, 2, 4)
    slab = jnp.concatenate([down, up.reshape(owned, 4, -1, LANES)], axis=2).transpose(1, 0, 2, 3)
    order_y = [yi, 1 - yi, yi, 1 - yi]
    order_c = [ci, ci, 1 - ci, 1 - ci]
    quarters = [y * 2 + c for y, c in zip(order_y, order_c)]
    part = [lax.dynamic_index_in_dim(slab, q, 0, keepdims=False) for q in quarters]
    diagonal = [(0, 3), (1, 2), (2, 1), (3, 0)]
    local = [part[0], swap(part[1], "y"), swap(part[2], "c"), lax.ppermute(part[3], ("y", "c"), diagonal)]

    shifts = sorted(range(1, zn), key=lambda s: -min(s, zn - s))
    whole, split = shifts[: max(zn - 3, 0)], shifts[max(zn - 3, 0) :]
    if not thin:
        blocks = [
            lax.dynamic_slice_in_dim(value_weight, lax.rem(ti + shift, tp) * cols, cols, 1)
            for shift in list(range(1, tp)) + [0]
        ]
        along_z = [value_weight] + [rotate(value_weight, "z", s) for s in whole]
        early_z = [[rotate(b, "z", s) for s in split] for b in blocks[:-1]]
        places = [lax.rem(zi - s + zn, zn) * 4 + q for q in quarters for s in [0] + whole]
        places += [lax.rem(zi - s + zn, zn) * 4 + q for q in quarters for s in split]

    def send_at(shift):
        return plan.send_at + (shift - 1) * here

    pays = pick(table, local, [[send_at(s) + k for k in range(PAIR)] for s in range(1, zn)])
    got = [rotate(p, "z", s) for s, p in zip(range(1, zn), pays)]

    base_parts = []
    if not thin:
        pays, along_z = together(pays, along_z)

        def spread(pieces):
            both = pieces + [swap(p, "y") for p in pieces]
            return both + [swap(p, "c") for p in both]

        common = spread(along_z)
        for i, pieces in enumerate(early_z):
            order = jnp.stack(places + [lax.rem(ti + i + 1, tp)])
            pieces = common + spread(pieces)
            base_parts.append(base_product(tokens, pieces, order, cols, BF, block_rows))
        got, base_parts, common = together(got, base_parts, common)

    spare = blank(((zn - 1) * (here - PAIR), *slab.shape[2:]))
    for s in range(1, zn):

        def extra(k, spare, s=s):
            (pay,) = pick(table, local, [[send_at(s)]], k)
            return lax.dynamic_update_slice_in_dim(spare, rotate(pay, "z", s), (s - 1) * (here - PAIR) + k - PAIR, 0)

        spare = lax.fori_loop(PAIR, jnp.maximum(table[plan.pair_at + s], PAIR), extra, spare)
    sources = local + got + [spare]

    def exchange(first, last):
        mine, theirs = pick(
            table,
            sources,
            [[plan.mine_at + j for j in range(first, last)], [plan.partner_at + j for j in range(first, last)]],
        )
        return mine, theirs

    more = (plan.most_chip - CHIP, *slab.shape[2:])

    def exchange_more():
        mine, theirs = exchange(CHIP, plan.most_chip)
        crossed = swap(theirs, "y")
        return [mine, crossed, swap(mine, "c"), swap(crossed, "c")]

    spares = lax.cond(table[plan.chip_at] > CHIP, exchange_more, lambda: [blank(more) for _ in range(4)])
    (table,), spares = together([table], spares)
    mine, theirs = exchange(0, CHIP)
    slot = table[plan.slot_at : plan.slot_at + FMAX]
    where = [jnp.concatenate([jnp.stack([quarters[i], quarters[i + 2]]), slot]) for i in range(2)]

    base_got = []
    if not thin:
        (mine, theirs), late = together([mine, theirs], [blocks[-1]])
    crossed = swap(theirs, "y")
    mine_c = swap(mine, "c")
    if not thin:
        base_got = [rotate(p, "tp", i + 1) for i, p in enumerate(base_parts)]
        late_z = [rotate(late[0], "z", s) for s in split]
        late_y = [swap(p, "y") for p in late_z]
    (rank,) = rank_product(tokens, [mine, mine_c], spares[0::2], where[0], None, quarter, block_rows)
    crossed_c = swap(crossed, "c")
    mains = [mine, crossed, mine_c, crossed_c]

    if thin:
        full = lax.all_gather(value_weight, ("z", "y", "c"), axis=0, tiled=True)
        product = jnp.dot(tokens, full, preferred_element_type=F32)
        base = lax.psum_scatter(product.astype(BF), "tp", scatter_dimension=1, tiled=True).astype(F32)
        base_got = [jnp.zeros(base.shape, BF)] * (tp - 1)
    else:
        pieces = late_z + late_y
        pieces = common + pieces + [swap(p, "c") for p in pieces]
        base = base_product(tokens, pieces, jnp.stack(places + [ti]), cols, F32, block_rows)

    rank, rank_bf = rank_product(tokens, mains[1::2], spares[1::2], where[1], rank, quarter, block_rows)
    rank_got = [rotate(rank_bf, "tp", s) for s in range(1, tp)]
    where = jnp.concatenate([jnp.stack(quarters), slot])
    return final_sum(rank, rank_got, base, base_got, mains, spares, where, quarter, block_rows)


def solution(mesh):
    tp, ad = mesh.shape["tp"], mesh.shape["ad"]
    fine = Mesh(mesh.devices.reshape(tp, ad // 4, 2, 2), ("tp", "z", "y", "c"))
    at = ("z", "y", "c")

    return jax.shard_map(
        body,
        mesh=fine,
        in_specs=(
            P(at, "tp"),
            P(("tp",) + at, None),
            P(at, "tp", None),
            P(at, None, "tp"),
            P(),
            P(),
            P(),
        ),
        out_specs=P(at, "tp"),
        check_vma=False,
    )
```
